32 devices in a mesh: dp: 4 (over x, core), ctx: 2 (over y), head: 4 (over z).
Axes of the slice: x: 2, y: 2, z: 4, core: 2. Of those that a mesh axis runs over, the one named last changes fastest.
Arguments:
- inputs: bfloat16 [16, 256, 1024], P('dp', 'ctx', 'head'), parts along dimension 0, may hold values from -6 to 6
- lengths: int32 [16], P('dp'), parts along dimension 0, may hold values from 1 to 640, 1024 in all
- proj_in: bfloat16 [1024, 4, 1024], P(None, None, 'head'), may hold values from -0.1875 to 0.1875
- proj_out: bfloat16 [1024, 1024], P('head'), may hold values from -0.1875 to 0.1875
Outputs:
- layer_out: bfloat16 [8, 2, 256, 1024], P(('dp', 'ctx'), None, None, 'head'), parts along dimension 0
The draws below stay inside these ranges and needn't reach their ends.
There are 4 independent parts, one for each index of `dp`. The reference program is written for one: setup_inputs(seed, part) draws one part's arguments, and reference() takes and returns one part's arrays. A program takes and returns all parts, laid end to end along the dimension named above; an argument that names none is the same for every part. Nothing has to cross between parts.
Inputs may be any that keep to these rules, and one draw needn't show every extreme that they name: The 4 histories lie end to end in the packed rows; the lengths sum to 1024 and the longest is exactly 640.
All inputs are finite; a program needn't handle non-finite values.
Results may differ from the reference program's by a relative error of at most 0.0055.
Values may be sent and summed in bfloat16 or wider, within the bound.
No kernel may reach another device: no remote copies, remote signals or barrier semaphores. Data moves between devices by JAX's collectives and lax.ppermute only.
A program may use at most 64 MiB of HBM per device.

```python
import math
import jax
import jax.numpy as jnp
import numpy as np
from jax import lax

D = 1024
HEADS = 8
HDIM = 128
USERS = 4
BLK = 256
BLOCKS = 4
TOTAL = 1024
LONGEST = 640


def steps_of(stream_key, extent, shards, low, largest):
    def one(dim, shards_of):
        draws = jax.random.uniform(jax.random.fold_in(jax.random.fold_in(stream_key, 6), dim), (shards_of,), jnp.float32, low / len(shards), largest / len(shards))
        return jnp.repeat(jnp.exp(draws), extent[dim] // shards_of).reshape((-1,) + (1,) * (len(extent) - dim - 1))

    gain = one(*shards[0])
    for cut in shards[1:]:
        gain = gain * one(*cut)
    return gain


def profile(number_of, total, limit, skew):
    loads = [(1 << 20) // math.isqrt(rank ** skew) + 1 for rank in range(2, number_of + 1)]
    spare, given = total - limit - (number_of - 1), [1] * (number_of - 1)
    while spare > 0:
        movable = [i for i in range(number_of - 1) if given[i] < limit]
        mass, remaining = sum([loads[i] for i in movable]), spare
        for i in movable:
            addition = min(limit - given[i], max(1, remaining * loads[i] // mass), spare)
            given[i] = given[i] + addition
            spare = spare - addition
    return np.array([limit] + given)


def ragged(key, count, total, most, lean):
    if count == 2:
        one = jax.random.randint(key, (), max(1, total - most), min(most, total - 1) + 1)
        return jnp.stack([one, total - one])
    tallies = jnp.asarray(profile(count, total, most, lean), jnp.int32)
    couples = (count - 1) // 2
    source_of, receiver = tallies[1:1 + 2 * couples:2], tallies[2:2 + 2 * couples:2]
    room = jnp.minimum(source_of - 1, most - receiver)
    passed = jax.random.randint(jax.random.fold_in(key, 1), (couples,), 0, 1 << 20) % (room + 1)
    tallies = tallies.at[1:1 + 2 * couples:2].set(source_of - passed).at[2:2 + 2 * couples:2].set(receiver + passed)
    return tallies[jax.random.permutation(jax.random.fold_in(key, 2), count)]


def noise(own_key, shape, width, bound, split=(), kind=jnp.bfloat16):
    loudness = steps_of(own_key, shape, split, -0.22, 0.18) if split else 1.0
    values = jax.random.normal(own_key, shape, jnp.float32) * width * loudness
    return jnp.minimum(jnp.maximum(values, -bound), bound).astype(kind)


def setup_inputs(seed: int = 0, part: int = 0) -> dict:
    key_of = jax.random.split(jax.random.key(seed), 5)
    own_keys = jax.random.split(jax.random.fold_in(key_of[4], part), 5)
    inputs = noise(own_keys[0], (BLOCKS, BLK, D), 1.0, 6.0, ((1, 2), (2, 4)))
    lengths = ragged(own_keys[1], USERS, TOTAL, LONGEST, 2).astype(jnp.int32)
    proj_in = noise(key_of[2], (D, 4, HEADS * HDIM), D ** -0.5, 0.1875, ((2, 4),))
    proj_out = noise(key_of[3], (HEADS * HDIM, D), (HEADS * HDIM) ** -0.5, 0.1875, ((0, 4),))
    return {"inputs": inputs, "lengths": lengths, "proj_in": proj_in, "proj_out": proj_out}


def layer_norm(values, epsilon):
    center = values - lax.optimization_barrier(jnp.mean(values, axis=-1, keepdims=True))
    spread = lax.optimization_barrier(jnp.mean(center * center, axis=-1, keepdims=True))
    return center * lax.rsqrt(spread + epsilon)

def reference(inputs, lengths, proj_in, proj_out):
    flat_rows = inputs.reshape(TOTAL, D).astype(jnp.float32)
    normed = layer_norm(flat_rows, 1e-06).astype(jnp.bfloat16)
    projected = jax.nn.silu(jnp.dot(normed, proj_in.reshape(D, -1), preferred_element_type=jnp.float32))
    projected = projected.astype(jnp.bfloat16).reshape(TOTAL, 4, HEADS, HDIM)
    gating = projected[:, 0]
    values = projected[:, 1].astype(jnp.float32)
    queries = projected[:, 2].astype(jnp.float32)
    keys_all = projected[:, 3].astype(jnp.float32)
    user_ends = jnp.cumsum(lengths).astype(jnp.int32)
    positions = jnp.arange(TOTAL, dtype=jnp.int32)
    user_of = lax.optimization_barrier(jnp.sum((positions[:, None] >= user_ends[None, :]).astype(jnp.int32), axis=1))
    query_block = math.gcd(TOTAL, 512)
    score_scale = 1.0 / math.sqrt(HDIM)

    def one_block(block_index):
        begin = (block_index * query_block).astype(jnp.int32)
        query_rows = lax.dynamic_slice_in_dim(queries, begin, query_block, 0)
        query_pos = lax.dynamic_slice_in_dim(positions, begin, query_block, 0)
        query_user = lax.dynamic_slice_in_dim(user_of, begin, query_block, 0)
        allowed = (query_user[:, None] == user_of[None, :]) & (positions[None, :] <= query_pos[:, None])
        scores = jnp.einsum('qhd,khd->hqk', query_rows, keys_all) * score_scale
        weights = jnp.where(allowed[None], jax.nn.silu(scores), 0.0).astype(jnp.bfloat16)
        return jnp.einsum('hqk,khd->qhd', weights.astype(jnp.float32), values)
    attended = lax.map(one_block, jnp.arange(TOTAL // query_block, dtype=jnp.int32))
    attended = attended.reshape(TOTAL, HEADS, HDIM)
    gate_prod = (layer_norm(attended, 1e-05) * gating.astype(jnp.float32)).astype(jnp.bfloat16)
    gate_prod = gate_prod.reshape(TOTAL, HEADS * HDIM)
    summed = flat_rows + jnp.dot(gate_prod, proj_out, preferred_element_type=jnp.float32)
    result = summed.astype(jnp.bfloat16).reshape(BLOCKS, BLK, D)
    half = BLOCKS // 2
    return jnp.stack([result[:half], result[half:][::-1]], axis=1)
```

```python
import functools
import math

import jax
import jax.numpy as jnp
from jax import lax
from jax.experimental import pallas as pl
from jax.experimental.pallas import tpu as pltpu
from jax.sharding import PartitionSpec as P

HDIM = 128
F32 = jnp.float32
BF16 = jnp.bfloat16


def layer_norm(values, epsilon):
    center = values - jnp.mean(values, axis=-1, keepdims=True)
    spread = jnp.mean(center * center, axis=-1, keepdims=True)
    return center * lax.rsqrt(spread + epsilon)


def silu_round(values):
    return jax.nn.silu(values).astype(jnp.bfloat16)


def ring_body(inputs, lengths, proj_in, proj_out):
    context_size = lax.axis_size("ctx")
    own_index = lax.axis_index("ctx")
    block_total, stripe, width_part = inputs.shape
    block_len = stripe * context_size
    row_count = 2 * block_len
    heads_dev = proj_in.shape[2] // HDIM
    reordered = jnp.stack([inputs[:context_size], inputs[context_size:][::-1]], axis=1)
    reordered = reordered.reshape(block_total, stripe, width_part)
    own_rows = lax.all_to_all(reordered, "ctx", split_axis=0, concat_axis=1, tiled=True)
    full_rows = lax.all_gather(own_rows, "head", axis=2, tiled=True)
    normed = layer_norm(full_rows.reshape(row_count, -1).astype(jnp.float32), 1e-06).astype(
        jnp.bfloat16
    )
    user_ends = jnp.cumsum(lengths)

    def segment(position):
        return jnp.sum((position[:, None] >= user_ends[None, :]).astype(jnp.int32), axis=1)

    offsets = jnp.arange(block_len, dtype=jnp.int32)
    own_blocks = jnp.stack([own_index, 2 * context_size - 1 - own_index])
    query_pos = (own_blocks[:, None] * block_len + offsets[None, :]).reshape(-1)
    query_seg = segment(query_pos)
    score_scale = 1.0 / math.sqrt(HDIM)
    projected = silu_round(
        jnp.einsum("rd,dgc->rgc", normed, proj_in, preferred_element_type=jnp.float32)
    )
    gating = projected[:, 0]
    queries = projected[:, 2]
    key_pair = (
        projected[:, 3].reshape(2, block_len, -1),
        projected[:, 1].reshape(2, block_len, -1),
    )

    def loader(shards, lead_row, tile_rows):
        key_rows = lax.dynamic_slice_in_dim(shards[0], lead_row, tile_rows, 0)
        value_rows = lax.dynamic_slice_in_dim(shards[1], lead_row, tile_rows, 0)
        return (
            key_rows.reshape(tile_rows * block_len, heads_dev, HDIM),
            value_rows.reshape(tile_rows * block_len, heads_dev, HDIM),
        )

    query_heads = queries.reshape(row_count, heads_dev, HDIM)
    zero_acc = jnp.zeros((row_count, heads_dev, HDIM), jnp.float32)
    shards = (
        lax.all_gather(key_pair[0], "ctx", axis=0, tiled=True),
        lax.all_gather(key_pair[1], "ctx", axis=0, tiled=True),
    )
    piece_rows = shards[0].shape[0]
    tile_rows = 4

    def one_tile(tile_index, partial_value):
        lead_row = tile_index * tile_rows
        listed = lead_row + jnp.arange(tile_rows, dtype=jnp.int32)
        holder = listed // 2
        block_ids = jnp.where(listed % 2 == 0, holder, 2 * context_size - 1 - holder)
        key_pos = (block_ids[:, None] * block_len + offsets[None, :]).reshape(-1)
        allowed = (query_seg[:, None] == segment(key_pos)[None, :]) & (
            key_pos[None, :] <= query_pos[:, None]
        )
        key_rows, value_rows = loader(shards, lead_row, tile_rows)
        scores = (
            jnp.einsum("qhd,khd->hqk", query_heads, key_rows, preferred_element_type=jnp.float32)
            * score_scale
        )
        weights = jnp.where(allowed[None], jax.nn.silu(scores), 0.0).astype(jnp.bfloat16)
        return partial_value + jnp.einsum(
            "hqk,khd->qhd", weights, value_rows, preferred_element_type=jnp.float32
        )

    attended = lax.fori_loop(0, piece_rows // tile_rows, one_tile, zero_acc)
    gate_prod = layer_norm(attended, 1e-05) * gating.reshape(row_count, heads_dev, HDIM).astype(
        jnp.float32
    )
    gate_prod = gate_prod.astype(jnp.bfloat16).reshape(row_count, -1)
    columns = lax.all_to_all(proj_out, "head", split_axis=1, concat_axis=0, tiled=True)
    summed = jnp.dot(
        lax.all_gather(gate_prod, "head", axis=1, tiled=True),
        columns,
        preferred_element_type=jnp.float32,
    )
    result = (own_rows.reshape(row_count, -1).astype(jnp.float32) + summed).astype(jnp.bfloat16)
    return result.reshape(1, 2, block_len, -1)


def half_silu(half):
    return half + half * jnp.tanh(half)


def project_kernel(ids, place, *refs):
    *shares, weight, keyval, gateq = refs
    pieces = []
    for ref in shares:
        pieces += [ref[k].astype(F32) for k in range(ref.shape[0])]
    part = pieces[0].shape[1]
    width = part * len(pieces)
    mean = sum(jnp.sum(p, axis=1, keepdims=True) for p in pieces) / width
    pieces = [p - mean for p in pieces]
    spread = sum(jnp.sum(p * p, axis=1, keepdims=True) for p in pieces) / width
    rscale = lax.rsqrt(spread + 1e-06)
    acc = None
    for share_id, piece in zip(ids, pieces):
        lead = pl.multiple_of((place[1] ^ share_id) * part, part)
        term = jnp.dot(
            (piece * rscale).astype(BF16), weight[pl.ds(lead, part), :], preferred_element_type=F32
        )
        acc = term if acc is None else acc + term
    done = half_silu(acc * 0.5).astype(BF16)
    group = done.shape[1] // 4
    gateq[0] = done[:, :group]
    keyval[0] = done[:, group : 2 * group]
    gateq[1] = done[:, 2 * group : 3 * group]
    keyval[1] = done[:, 3 * group :]


def attend_kernel(chunk, chunk_blocks, stripe, send_ids, keep_ids, place, lengths, *refs):
    *keyvals, gateq, weight, sent, kept = refs
    rows, cols = gateq.shape[1:]
    block_len = 2 * stripe
    own = place[0]

    def positions(shape, dim, which, side):
        offset = lax.broadcasted_iota(jnp.int32, shape, dim)
        block, inner = offset // stripe, offset % stripe
        return (which * chunk_blocks + block) * block_len + side * stripe + inner

    query_pos = positions((rows, 1), 0, chunk, own)
    start = jnp.zeros((rows, 1), jnp.int32)
    end = jnp.int32(0)
    for user in range(lengths.shape[0]):
        end = end + lengths[user]
        start = jnp.where(query_pos >= end, end, start)
    masks = []
    for index in range(len(keyvals)):
        key_pos = positions((1, rows), 1, index // 2, own if index % 2 == 0 else 1 - own)
        masks.append((key_pos <= query_pos) & (key_pos >= start))
    scale = 0.5 / math.sqrt(HDIM)
    gated = []
    for head in range(cols // HDIM):
        lanes = slice(head * HDIM, (head + 1) * HDIM)
        query = gateq[1, :, lanes]
        total = None
        for mask, ref in zip(masks, keyvals):
            scores = lax.dot_general(
                query, ref[1, :, lanes], (((1,), (1,)), ((), ())), preferred_element_type=F32
            )
            weights = jnp.where(mask, half_silu(scores * scale), 0.0).astype(BF16)
            term = jnp.dot(weights, ref[0, :, lanes], preferred_element_type=F32)
            total = term if total is None else total + term
        total = total - jnp.mean(total, axis=1, keepdims=True)
        spread = jnp.mean(total * total, axis=1, keepdims=True)
        total = total * lax.rsqrt(spread + 1e-05)
        gated.append((total * gateq[0, :, lanes].astype(F32)).astype(BF16))
    gated = jnp.concatenate(gated, axis=1)
    width_part = sent.shape[2]
    for target, listed in ((sent, send_ids), (kept, keep_ids)):
        for slot, share_id in enumerate(listed):
            lead = pl.multiple_of((place[1] ^ share_id) * width_part, width_part)
            product = jnp.dot(gated, weight[:, pl.ds(lead, width_part)], preferred_element_type=F32)
            target[slot] = product.astype(target.dtype)


def whole(memory_space=pltpu.VMEM):
    return pl.BlockSpec(memory_space=memory_space)


def pair_body(inputs, lengths, proj_in, proj_out):
    head_size = lax.axis_size("head")
    own = lax.axis_index("ctx")
    block_total, stripe, part = inputs.shape
    chunk_blocks = block_total // 2
    rows = chunk_blocks * stripe
    cols = proj_in.shape[2]
    place = jnp.stack([own, lax.axis_index("head")]).astype(jnp.int32)
    weight_in = proj_in.reshape(proj_in.shape[0], -1)
    bits = [1 << k for k in range(head_size.bit_length() - 1)]

    def over_head(value, bit):
        return lax.ppermute(value, "head", [(i, i ^ bit) for i in range(head_size)])

    def over_ctx(value):
        return lax.ppermute(value, "ctx", [(0, 1), (1, 0)])

    def across(value, bit):
        pairs = [
            (c * head_size + i, (1 - c) * head_size + (i ^ bit))
            for c in range(2)
            for i in range(head_size)
        ]
        return lax.ppermute(value, ("ctx", "head"), pairs)

    chunks = [inputs[:chunk_blocks].reshape(1, rows, part), inputs[chunk_blocks:].reshape(1, rows, part)]

    def gather(own_share):
        shares, ids = [own_share], [0]
        for bit in reversed(bits):
            packed = shares[0] if len(shares) == 1 else jnp.concatenate(shares, axis=0)
            shares.append(over_head(packed, bit))
            ids += [i ^ bit for i in ids]
        return shares, ids

    def project(shares, ids):
        size = jax.ShapeDtypeStruct((2, rows, cols), BF16)

        return pl.pallas_call(
            functools.partial(project_kernel, ids),
            name="project",
            out_shape=(size, size),
            in_specs=[whole(pltpu.SMEM)] + [whole()] * (len(shares) + 1),
            out_specs=(whole(), whole()),
            cost_estimate=pl.CostEstimate(
                flops=2 * rows * weight_in.size,
                bytes_accessed=2 * weight_in.size,
                transcendentals=rows * 4 * cols,
            ),
        )(place, *shares, weight_in)

    send_ids = [i for i in range(head_size) if i & 1]
    keep_ids = [i for i in range(head_size) if not i & 1]

    def attend(chunk, keyvals, gateq):
        slots = head_size // 2
        return pl.pallas_call(
            functools.partial(attend_kernel, chunk, chunk_blocks, stripe, send_ids, keep_ids),
            name="attend",
            out_shape=(
                jax.ShapeDtypeStruct((slots, rows, part), BF16),
                jax.ShapeDtypeStruct((slots, rows, part), F32),
            ),
            in_specs=[whole(pltpu.SMEM)] * 2 + [whole()] * (len(keyvals) + 2),
            out_specs=(whole(), whole()),
            cost_estimate=pl.CostEstimate(
                flops=4 * rows * rows * cols * len(keyvals) + 2 * rows * proj_out.size,
                bytes_accessed=2 * proj_out.size,
                transcendentals=rows * rows * len(keyvals) * (cols // HDIM),
            ),
        )(place, lengths, *keyvals, gateq, proj_out)

    keyvals, sums = [], []
    for chunk, own_share in enumerate(chunks):
        shares, ids = gather(own_share)
        keyval, gateq = project(shares, ids)
        keyvals += [keyval, over_ctx(keyval)]
        sent, kept = attend(chunk, keyvals, gateq)
        kept = kept + over_head(sent, 1).astype(F32)
        for bit in bits[1:-1]:
            kept = kept[0::2] + over_head(kept[1::2].astype(BF16), bit).astype(F32)
        sums.append(kept)
    last = bits[-1]

    def split(value, which):
        return lax.dynamic_index_in_dim(value.reshape(chunk_blocks, stripe, part), which, 0, keepdims=False)

    low, high = sums
    full = low[0] + over_head(low[1].astype(BF16), last).astype(F32) + chunks[0][0].astype(F32)
    full = full.astype(BF16)
    stay_low, move_low = split(full, own), split(full, 1 - own)
    base = high[0] + chunks[1][0].astype(F32)
    away = high[1].astype(BF16)
    stay_high = split(base, 1 - own) + over_head(split(away, 1 - own), last).astype(F32)
    turned = across(split(away, own), last).astype(F32)
    moved = over_ctx(jnp.stack([move_low, split(base, own).astype(BF16)]))
    stay = jnp.stack([stay_low, stay_high.astype(BF16)])
    come = jnp.stack([moved[0], (moved[1].astype(F32) + turned).astype(BF16)])
    result = jnp.where(
        own == 0, jnp.concatenate([stay, come], axis=1), jnp.concatenate([come, stay], axis=1)
    )
    return result[None]


def body(inputs, lengths, proj_in, proj_out):
    context_size = lax.axis_size("ctx")
    head_size = lax.axis_size("head")
    paired = context_size == 2 and inputs.shape[0] == 2 * context_size
    if paired and head_size > 2 and head_size & (head_size - 1) == 0:
        return pair_body(inputs, lengths, proj_in, proj_out)
    return ring_body(inputs, lengths, proj_in, proj_out)


def solution(mesh):
    return jax.shard_map(
        body,
        mesh=mesh,
        in_specs=(P("dp", "ctx", "head"), P("dp"), P(None, None, "head"), P("head", None)),
        out_specs=P(("dp", "ctx"), None, None, "head"),
        check_vma=False,
    )
```

```python
import functools
import math

import jax
import jax.numpy as jnp
from jax import lax
from jax.experimental import pallas as pl
from jax.experimental.pallas import tpu as pltpu
from jax.sharding import PartitionSpec as P


HDIM = 128
GRANT = 16 << 20
F32 = jnp.float32
BF16 = jnp.bfloat16


def layer_norm(values, epsilon):
    center = values - jnp.mean(values, axis=-1, keepdims=True)
    spread = jnp.mean(center * center, axis=-1, keepdims=True)
    return center * lax.rsqrt(spread + epsilon)


def silu_round(values):
    return jax.nn.silu(values).astype(jnp.bfloat16)


def ring_body(inputs, lengths, proj_in, proj_out):
    context_size = lax.axis_size("ctx")
    own_index = lax.axis_index("ctx")
    block_total, stripe, width_part = inputs.shape
    block_len = stripe * context_size
    row_count = 2 * block_len
    heads_dev = proj_in.shape[2] // HDIM
    reordered = jnp.stack([inputs[:context_size], inputs[context_size:][::-1]], axis=1)
    reordered = reordered.reshape(block_total, stripe, width_part)
    own_rows = lax.all_to_all(reordered, "ctx", split_axis=0, concat_axis=1, tiled=True)
    full_rows = lax.all_gather(own_rows, "head", axis=2, tiled=True)
    normed = layer_norm(full_rows.reshape(row_count, -1).astype(jnp.float32), 1e-06).astype(
        jnp.bfloat16
    )
    user_ends = jnp.cumsum(lengths)

    def segment(position):
        return jnp.sum((position[:, None] >= user_ends[None, :]).astype(jnp.int32), axis=1)

    offsets = jnp.arange(block_len, dtype=jnp.int32)
    own_blocks = jnp.stack([own_index, 2 * context_size - 1 - own_index])
    query_pos = (own_blocks[:, None] * block_len + offsets[None, :]).reshape(-1)
    query_seg = segment(query_pos)
    score_scale = 1.0 / math.sqrt(HDIM)
    projected = silu_round(
        jnp.einsum("rd,dgc->rgc", normed, proj_in, preferred_element_type=jnp.float32)
    )
    gating = projected[:, 0]
    queries = projected[:, 2]
    key_pair = (
        projected[:, 3].reshape(2, block_len, -1),
        projected[:, 1].reshape(2, block_len, -1),
    )

    def loader(shards, lead_row, tile_rows):
        key_rows = lax.dynamic_slice_in_dim(shards[0], lead_row, tile_rows, 0)
        value_rows = lax.dynamic_slice_in_dim(shards[1], lead_row, tile_rows, 0)
        return (
            key_rows.reshape(tile_rows * block_len, heads_dev, HDIM),
            value_rows.reshape(tile_rows * block_len, heads_dev, HDIM),
        )

    query_heads = queries.reshape(row_count, heads_dev, HDIM)
    zero_acc = jnp.zeros((row_count, heads_dev, HDIM), jnp.float32)
    shards = (
        lax.all_gather(key_pair[0], "ctx", axis=0, tiled=True),
        lax.all_gather(key_pair[1], "ctx", axis=0, tiled=True),
    )
    piece_rows = shards[0].shape[0]
    tile_rows = 4

    def one_tile(tile_index, partial_value):
        lead_row = tile_index * tile_rows
        listed = lead_row + jnp.arange(tile_rows, dtype=jnp.int32)
        holder = listed // 2
        block_ids = jnp.where(listed % 2 == 0, holder, 2 * context_size - 1 - holder)
        key_pos = (block_ids[:, None] * block_len + offsets[None, :]).reshape(-1)
        allowed = (query_seg[:, None] == segment(key_pos)[None, :]) & (
            key_pos[None, :] <= query_pos[:, None]
        )
        key_rows, value_rows = loader(shards, lead_row, tile_rows)
        scores = (
            jnp.einsum("qhd,khd->hqk", query_heads, key_rows, preferred_element_type=jnp.float32)
            * score_scale
        )
        weights = jnp.where(allowed[None], jax.nn.silu(scores), 0.0).astype(jnp.bfloat16)
        return partial_value + jnp.einsum(
            "hqk,khd->qhd", weights, value_rows, preferred_element_type=jnp.float32
        )

    attended = lax.fori_loop(0, piece_rows // tile_rows, one_tile, zero_acc)
    gate_prod = layer_norm(attended, 1e-05) * gating.reshape(row_count, heads_dev, HDIM).astype(
        jnp.float32
    )
    gate_prod = gate_prod.astype(jnp.bfloat16).reshape(row_count, -1)
    columns = lax.all_to_all(proj_out, "head", split_axis=1, concat_axis=0, tiled=True)
    summed = jnp.dot(
        lax.all_gather(gate_prod, "head", axis=1, tiled=True),
        columns,
        preferred_element_type=jnp.float32,
    )
    result = (own_rows.reshape(row_count, -1).astype(jnp.float32) + summed).astype(jnp.bfloat16)
    return result.reshape(1, 2, block_len, -1)


def half_silu(half):
    return half + half * jnp.tanh(half)


def project_kernel(place, own, near, far, mid, relay, weight, keyval, gateq):
    pieces = [own[0].astype(F32), near[0].astype(F32), far[0].astype(F32)]
    pieces.append(mid[0].astype(F32) + relay[0].astype(F32))
    part = pieces[0].shape[1]
    width = part * len(pieces)
    mean = sum(jnp.sum(p, axis=1, keepdims=True) for p in pieces) / width
    pieces = [p - mean for p in pieces]
    spread = sum(jnp.sum(p * p, axis=1, keepdims=True) for p in pieces) / width
    rscale = lax.rsqrt(spread + 1e-06)
    acc = None
    for share_id, piece in enumerate(pieces):
        lead = pl.multiple_of((place[1] ^ share_id) * part, part)
        term = jnp.dot(
            (piece * rscale).astype(BF16), weight[pl.ds(lead, part), :], preferred_element_type=F32
        )
        acc = term if acc is None else acc + term
    done = half_silu(acc * 0.5).astype(BF16)
    group = done.shape[1] // 4
    gateq[0] = done[:, :group]
    keyval[0] = done[:, group : 2 * group]
    gateq[1] = done[:, 2 * group : 3 * group]
    keyval[1] = done[:, 3 * group :]


def weighted_values(plan, place, lengths, gateq, keyvals, first=None):
    chunk, chunk_blocks, stripe, origins = plan
    rows, cols = gateq.shape[1:]
    block_len = 2 * stripe

    def positions(shape, dim, which, side):
        offset = lax.broadcasted_iota(jnp.int32, shape, dim)
        block, inner = offset // stripe, offset % stripe
        return (which * chunk_blocks + block) * block_len + side * stripe + inner

    query_pos = positions((rows, 1), 0, chunk, place[0])
    start = jnp.zeros((rows, 1), jnp.int32)
    end = jnp.int32(0)
    for user in range(lengths.shape[0]):
        end = end + lengths[user]
        start = jnp.where(query_pos >= end, end, start)
    masks = []
    for which, side in origins:
        key_pos = positions((1, rows), 1, which, place[0] ^ side)
        masks.append((key_pos <= query_pos) & (key_pos >= start))
    scale = 0.5 / math.sqrt(HDIM)
    totals = []
    for head in range(cols // HDIM):
        lanes = slice(head * HDIM, (head + 1) * HDIM)
        query = gateq[1, :, lanes]
        total = None if first is None else first[:, lanes]
        for mask, ref in zip(masks, keyvals):
            scores = lax.dot_general(
                query, ref[1, :, lanes], (((1,), (1,)), ((), ())), preferred_element_type=F32
            )
            weights = jnp.where(mask, half_silu(scores * scale), 0.0).astype(BF16)
            term = jnp.dot(weights, ref[0, :, lanes], preferred_element_type=F32)
            total = term if total is None else total + term
        totals.append(total)
    return totals


def near_kernel(plan, place, lengths, *refs):
    *keyvals, gateq, partial = refs
    totals = weighted_values(plan, place, lengths, gateq, keyvals)
    for head, total in enumerate(totals):
        partial[:, head * HDIM : (head + 1) * HDIM] = total


def attend_kernel(plan, splits, place, lengths, keyval, partial, gateq, weight, share, *refs):
    *outputs, held = refs
    chunk, _, stripe, _ = plan
    part = share.shape[2]
    totals = weighted_values(plan, place, lengths, gateq, [keyval], partial)
    for head, total in enumerate(totals):
        lanes = slice(head * HDIM, (head + 1) * HDIM)
        total = total - jnp.mean(total, axis=1, keepdims=True)
        spread = jnp.mean(total * total, axis=1, keepdims=True)
        total = total * lax.rsqrt(spread + 1e-05)
        held[:, lanes] = (total * gateq[0, :, lanes].astype(F32)).astype(BF16)
    away = place[0] if chunk == 1 else 1 - place[0]
    leads = [pl.multiple_of(away * stripe, stripe), pl.multiple_of((1 - away) * stripe, stripe)]
    gated = [held[pl.ds(lead, stripe), :] for lead in leads]
    shares = [share[0, pl.ds(lead, stripe), :] for lead in leads]
    if splits == 1:
        gated, shares = [jnp.concatenate(gated, axis=0)], [jnp.concatenate(shares, axis=0)]
    for index in range(splits):
        sent, kept = outputs[2 * index : 2 * index + 2]
        for share_id in (1, 3, 2, 0):
            lead = pl.multiple_of((place[1] ^ share_id) * part, part)
            product = jnp.dot(
                gated[index], weight[:, pl.ds(lead, part)], preferred_element_type=F32
            )
            if share_id == 0:
                product = product + shares[index].astype(F32)
            target = sent if share_id & 1 else kept
            target[share_id >> 1] = product.astype(target.dtype)


def whole(memory_space=pltpu.VMEM):
    return pl.BlockSpec(memory_space=memory_space)


def pair_body(inputs, lengths, proj_in, proj_out):
    head_size = lax.axis_size("head")
    own = lax.axis_index("ctx")
    block_total, stripe, part = inputs.shape
    chunk_blocks = block_total // 2
    rows = chunk_blocks * stripe
    cols = proj_in.shape[2]
    place = jnp.stack([own, lax.axis_index("head")]).astype(jnp.int32)
    weight_in = proj_in.reshape(proj_in.shape[0], -1)

    def over_head(value, pairs):
        if isinstance(pairs, int):
            pairs = [(i, i ^ pairs) for i in range(head_size)]
        return lax.ppermute(value, "head", pairs)

    def over_ctx(value):
        return lax.ppermute(value, "ctx", [(0, 1), (1, 0)])

    def kernel_call(function, outs, args, scalars, cost, scratch=()):
        return pl.pallas_call(
            function,
            compiler_params=pltpu.CompilerParams(vmem_limit_bytes=GRANT),
            out_shape=tuple(jax.ShapeDtypeStruct(*out) for out in outs),
            in_specs=[whole(pltpu.SMEM)] * scalars + [whole()] * (len(args) - scalars),
            out_specs=tuple(whole() for _ in outs),
            scratch_shapes=scratch,
            cost_estimate=cost,
        )(*args)

    def cost(flops, transcendentals):
        return pl.CostEstimate(flops=flops, bytes_accessed=1 << 20, transcendentals=transcendentals)

    inner = [(1, 2), (2, 1)]
    outer = [(1, 0), (2, 3)]

    def gather(own_share):
        far = over_head(own_share, 2)
        near = over_head(own_share, 1)
        mid = over_head(own_share, inner)
        relay = over_head(far, outer)
        return own_share, near, far, mid, relay

    def project(shares):
        size = ((2, rows, cols), BF16)
        return kernel_call(
            project_kernel,
            (size, size),
            (place, *shares, weight_in),
            1,
            cost(2 * rows * weight_in.size, rows * 4 * cols),
        )

    def near_part(chunk, origins, keyvals, gateq):
        count = len(keyvals)
        return kernel_call(
            functools.partial(near_kernel, (chunk, chunk_blocks, stripe, origins)),
            (((rows, cols), F32),),
            (place, lengths, *keyvals, gateq),
            2,
            cost(4 * rows * rows * cols * count, rows * rows * count * (cols // HDIM)),
        )[0]

    def attend(chunk, keyval, partial, gateq, share, splits):
        size = (2, rows // splits, part)
        return kernel_call(
            functools.partial(
                attend_kernel, (chunk, chunk_blocks, stripe, [(chunk, 1)]), splits
            ),
            ((size, BF16), (size, F32)) * splits,
            (place, lengths, keyval, partial, gateq, proj_out, share),
            2,
            cost(4 * rows * rows * cols + 2 * rows * proj_out.size, rows * rows * (cols // HDIM)),
            [pltpu.VMEM((rows, cols), BF16)],
        )

    def total(sent, kept):
        kept = kept + over_head(sent, 1).astype(F32)
        far = over_head(kept[1].astype(BF16), 2)
        return (kept[0] + far.astype(F32)).astype(BF16)

    chunks = [inputs[:chunk_blocks].reshape(1, rows, part), inputs[chunk_blocks:].reshape(1, rows, part)]
    low = gather(chunks[0])
    low_keyval, low_gateq = project(low)
    low_other = over_ctx(low_keyval)
    high = gather(chunks[1])
    high_keyval, high_gateq = project(high)
    high_other = over_ctx(high_keyval)
    low_first = near_part(0, [(0, 0)], [low_keyval], low_gateq)
    sent, kept = attend(0, low_other, low_first, low_gateq, chunks[0], 1)
    low_done = total(sent, kept)
    origins = [(0, 0), (0, 1), (1, 0)]
    high_first = near_part(1, origins, [low_keyval, low_other, high_keyval], high_gateq)
    sent, kept, sent_stay, kept_stay = attend(1, high_other, high_first, high_gateq, chunks[1], 2)
    high_move = total(sent, kept)
    high_stay = total(sent_stay, kept_stay)
    come = over_ctx(jnp.stack([low_done[:stripe], high_move]))
    stay = jnp.stack([low_done[stripe:], high_stay])
    result = jnp.where(
        own == 0, jnp.concatenate([stay, come], axis=1), jnp.concatenate([come, stay], axis=1)
    )
    return result[None]


def body(inputs, lengths, proj_in, proj_out):
    context_size = lax.axis_size("ctx")
    head_size = lax.axis_size("head")
    paired = context_size == 2 and inputs.shape[0] == 2 * context_size
    if paired and head_size == 4:
        return pair_body(inputs, lengths, proj_in, proj_out)
    return ring_body(inputs, lengths, proj_in, proj_out)


def solution(mesh):
    return jax.shard_map(
        body,
        mesh=mesh,
        in_specs=(P("dp", "ctx", "head"), P("dp"), P(None, None, "head"), P("head", None)),
        out_specs=P(("dp", "ctx"), None, None, "head"),
        check_vma=False,
    )
```

```python
import functools
import math

import jax
import jax.numpy as jnp
from jax import lax
from jax.experimental import pallas as pl
from jax.experimental.pallas import tpu as pltpu
from jax.sharding import PartitionSpec as P


HDIM = 128
GRANT = 16 << 20
F32 = jnp.float32
BF16 = jnp.bfloat16


def layer_norm(values, epsilon):
    center = values - jnp.mean(values, axis=-1, keepdims=True)
    spread = jnp.mean(center * center, axis=-1, keepdims=True)
    return center * lax.rsqrt(spread + epsilon)


def silu_round(values):
    return jax.nn.silu(values).astype(jnp.bfloat16)


def ring_body(inputs, lengths, proj_in, proj_out):
    context_size = lax.axis_size("ctx")
    own_index = lax.axis_index("ctx")
    block_total, stripe, width_part = inputs.shape
    block_len = stripe * context_size
    row_count = 2 * block_len
    heads_dev = proj_in.shape[2] // HDIM
    reordered = jnp.stack([inputs[:context_size], inputs[context_size:][::-1]], axis=1)
    reordered = reordered.reshape(block_total, stripe, width_part)
    own_rows = lax.all_to_all(reordered, "ctx", split_axis=0, concat_axis=1, tiled=True)
    full_rows = lax.all_gather(own_rows, "head", axis=2, tiled=True)
    normed = layer_norm(full_rows.reshape(row_count, -1).astype(jnp.float32), 1e-06).astype(
        jnp.bfloat16
    )
    user_ends = jnp.cumsum(lengths)

    def segment(position):
        return jnp.sum((position[:, None] >= user_ends[None, :]).astype(jnp.int32), axis=1)

    offsets = jnp.arange(block_len, dtype=jnp.int32)
    own_blocks = jnp.stack([own_index, 2 * context_size - 1 - own_index])
    query_pos = (own_blocks[:, None] * block_len + offsets[None, :]).reshape(-1)
    query_seg = segment(query_pos)
    score_scale = 1.0 / math.sqrt(HDIM)
    projected = silu_round(
        jnp.einsum("rd,dgc->rgc", normed, proj_in, preferred_element_type=jnp.float32)
    )
    gating = projected[:, 0]
    queries = projected[:, 2]
    key_pair = (
        projected[:, 3].reshape(2, block_len, -1),
        projected[:, 1].reshape(2, block_len, -1),
    )

    def loader(shards, lead_row, tile_rows):
        key_rows = lax.dynamic_slice_in_dim(shards[0], lead_row, tile_rows, 0)
        value_rows = lax.dynamic_slice_in_dim(shards[1], lead_row, tile_rows, 0)
        return (
            key_rows.reshape(tile_rows * block_len, heads_dev, HDIM),
            value_rows.reshape(tile_rows * block_len, heads_dev, HDIM),
        )

    query_heads = queries.reshape(row_count, heads_dev, HDIM)
    zero_acc = jnp.zeros((row_count, heads_dev, HDIM), jnp.float32)
    shards = (
        lax.all_gather(key_pair[0], "ctx", axis=0, tiled=True),
        lax.all_gather(key_pair[1], "ctx", axis=0, tiled=True),
    )
    piece_rows = shards[0].shape[0]
    tile_rows = 4

    def one_tile(tile_index, partial_value):
        lead_row = tile_index * tile_rows
        listed = lead_row + jnp.arange(tile_rows, dtype=jnp.int32)
        holder = listed // 2
        block_ids = jnp.where(listed % 2 == 0, holder, 2 * context_size - 1 - holder)
        key_pos = (block_ids[:, None] * block_len + offsets[None, :]).reshape(-1)
        allowed = (query_seg[:, None] == segment(key_pos)[None, :]) & (
            key_pos[None, :] <= query_pos[:, None]
        )
        key_rows, value_rows = loader(shards, lead_row, tile_rows)
        scores = (
            jnp.einsum("qhd,khd->hqk", query_heads, key_rows, preferred_element_type=jnp.float32)
            * score_scale
        )
        weights = jnp.where(allowed[None], jax.nn.silu(scores), 0.0).astype(jnp.bfloat16)
        return partial_value + jnp.einsum(
            "hqk,khd->qhd", weights, value_rows, preferred_element_type=jnp.float32
        )

    attended = lax.fori_loop(0, piece_rows // tile_rows, one_tile, zero_acc)
    gate_prod = layer_norm(attended, 1e-05) * gating.reshape(row_count, heads_dev, HDIM).astype(
        jnp.float32
    )
    gate_prod = gate_prod.astype(jnp.bfloat16).reshape(row_count, -1)
    columns = lax.all_to_all(proj_out, "head", split_axis=1, concat_axis=0, tiled=True)
    summed = jnp.dot(
        lax.all_gather(gate_prod, "head", axis=1, tiled=True),
        columns,
        preferred_element_type=jnp.float32,
    )
    result = (own_rows.reshape(row_count, -1).astype(jnp.float32) + summed).astype(jnp.bfloat16)
    return result.reshape(1, 2, block_len, -1)


def half_silu(half):
    return half + half * jnp.tanh(half)


def project_kernel(place, own, near, far, mid, relay, weight, keyval, gateq):
    pieces = [own[0].astype(F32), near[0].astype(F32), far[0].astype(F32)]
    pieces.append(mid[0].astype(F32) + relay[0].astype(F32))
    part = pieces[0].shape[1]
    width = part * len(pieces)
    mean = sum(jnp.sum(p, axis=1, keepdims=True) for p in pieces) / width
    pieces = [p - mean for p in pieces]
    spread = sum(jnp.sum(p * p, axis=1, keepdims=True) for p in pieces) / width
    rscale = lax.rsqrt(spread + 1e-06)
    acc = None
    for share_id, piece in enumerate(pieces):
        lead = pl.multiple_of((place[1] ^ share_id) * part, part)
        term = jnp.dot(
            (piece * rscale).astype(BF16), weight[pl.ds(lead, part), :], preferred_element_type=F32
        )
        acc = term if acc is None else acc + term
    done = half_silu(acc * 0.5).astype(BF16)
    group = done.shape[1] // 4
    gateq[0] = done[:, :group]
    keyval[0] = done[:, group : 2 * group]
    gateq[1] = done[:, 2 * group : 3 * group]
    keyval[1] = done[:, 3 * group :]


def weighted_values(plan, place, lengths, gateq, keyvals, first=None):
    chunk, stripe, origins = plan
    rows, cols = gateq.shape[1:]

    def positions(shape, dim, which, side):
        offset = lax.broadcasted_iota(jnp.int32, shape, dim)
        block = side if which == 0 else 3 - side
        inner = jnp.where(offset < stripe, offset + side * stripe, offset - side * stripe)
        return block * rows + inner

    query_pos = positions((rows, 1), 0, chunk, place[0])
    start = jnp.zeros((rows, 1), jnp.int32)
    end = jnp.int32(0)
    for user in range(lengths.shape[0]):
        end = end + lengths[user]
        start = jnp.where(query_pos >= end, end, start)
    masks = []
    for which, side in origins:
        key_pos = positions((1, rows), 1, which, place[0] ^ side)
        masks.append((key_pos <= query_pos) & (key_pos >= start))
    scale = 0.5 / math.sqrt(HDIM)
    totals = []
    for head in range(cols // HDIM):
        lanes = slice(head * HDIM, (head + 1) * HDIM)
        query = gateq[1, :, lanes]
        total = None if first is None else first[:, lanes]
        for mask, ref in zip(masks, keyvals):
            scores = lax.dot_general(
                query, ref[1, :, lanes], (((1,), (1,)), ((), ())), preferred_element_type=F32
            )
            weights = jnp.where(mask, half_silu(scores * scale), 0.0).astype(BF16)
            term = jnp.dot(weights, ref[0, :, lanes], preferred_element_type=F32)
            total = term if total is None else total + term
        totals.append(total)
    return totals


def near_kernel(plan, place, lengths, *refs):
    *keyvals, gateq, partial = refs
    totals = weighted_values(plan, place, lengths, gateq, keyvals)
    for head, total in enumerate(totals):
        partial[:, head * HDIM : (head + 1) * HDIM] = total


def attend_kernel(plan, place, lengths, keyval, partial, gateq, weight, share, *refs):
    *outputs, held = refs
    part = share.shape[2]
    totals = weighted_values(plan, place, lengths, gateq, [keyval], partial)
    for head, total in enumerate(totals):
        lanes = slice(head * HDIM, (head + 1) * HDIM)
        total = total - jnp.mean(total, axis=1, keepdims=True)
        spread = jnp.mean(total * total, axis=1, keepdims=True)
        total = total * lax.rsqrt(spread + 1e-05)
        held[:, lanes] = (total * gateq[0, :, lanes].astype(F32)).astype(BF16)
    gated = held[...]
    for share_id in (2, 3, 1, 0):
        lead = pl.multiple_of((place[1] ^ share_id) * part, part)
        product = jnp.dot(gated, weight[:, pl.ds(lead, part)], preferred_element_type=F32)
        if share_id == 0:
            product = product + share[0].astype(F32)
        outputs[share_id][...] = product.astype(outputs[share_id].dtype)


def whole(memory_space=pltpu.VMEM):
    return pl.BlockSpec(memory_space=memory_space)


def pair_body(inputs, lengths, proj_in, proj_out):
    head_size = lax.axis_size("head")
    own = lax.axis_index("ctx")
    _, stripe, part = inputs.shape
    rows = 2 * stripe
    cols = proj_in.shape[2]
    place = jnp.stack([own, lax.axis_index("head")]).astype(jnp.int32)
    weight_in = proj_in.reshape(proj_in.shape[0], -1)

    def over_head(value, pairs):
        if isinstance(pairs, int):
            pairs = [(i, i ^ pairs) for i in range(head_size)]
        return lax.ppermute(value, "head", pairs)

    def over_ctx(value):
        return lax.ppermute(value, "ctx", [(0, 1), (1, 0)])

    def kernel_call(function, outs, args, scalars, cost, scratch=()):
        return pl.pallas_call(
            function,
            compiler_params=pltpu.CompilerParams(vmem_limit_bytes=GRANT),
            out_shape=tuple(jax.ShapeDtypeStruct(*out) for out in outs),
            in_specs=[whole(pltpu.SMEM)] * scalars + [whole()] * (len(args) - scalars),
            out_specs=tuple(whole() for _ in outs),
            scratch_shapes=scratch,
            cost_estimate=cost,
        )(*args)

    def cost(flops, transcendentals):
        return pl.CostEstimate(flops=flops, bytes_accessed=1 << 20, transcendentals=transcendentals)

    weights = []
    inner = [(1, 2), (2, 1)]
    outer = [(1, 0), (2, 3)]

    def settle(chunk):
        stay = own if chunk == 0 else 1 - own
        blocks = inputs[chunk * 2 : chunk * 2 + 2]
        home = lax.dynamic_index_in_dim(blocks, stay, 0, keepdims=True)
        away = lax.dynamic_index_in_dim(blocks, 1 - stay, 0, keepdims=True)
        return jnp.concatenate([home, over_ctx(away)], axis=1)

    def gather(own_share, tag):
        far = over_head(own_share, 2)
        near = over_head(own_share, 1)
        mid = over_head(own_share, inner)
        if tag == "a":
            far, weight = lax.optimization_barrier((far, weight_in))
            weights.append(weight)
        relay = over_head(far, outer)
        return own_share, near, far, mid, relay

    def project(shares):
        size = ((2, rows, cols), BF16)
        return kernel_call(
            project_kernel,
            (size, size),
            (place, *shares, weights[0]),
            1,
            cost(2 * rows * weight_in.size, rows * 4 * cols),
        )

    def near_part(chunk, origins, keyvals, gateq):
        count = len(keyvals)
        return kernel_call(
            functools.partial(near_kernel, (chunk, stripe, origins)),
            (((rows, cols), F32),),
            (place, lengths, *keyvals, gateq),
            2,
            cost(4 * rows * rows * cols * count, rows * rows * count * (cols // HDIM)),
        )[0]

    def attend(chunk, keyval, partial, gateq, share):
        size = (rows, part)
        return kernel_call(
            functools.partial(attend_kernel, (chunk, stripe, [(chunk, 1)])),
            ((size, F32),) + ((size, BF16),) * 3,
            (place, lengths, keyval, partial, gateq, proj_out, share),
            2,
            cost(4 * rows * rows * cols + 2 * rows * proj_out.size, rows * rows * (cols // HDIM)),
            [pltpu.VMEM((rows, cols), BF16)],
        )

    def total(kept, *sent):
        for share_id in (2, 3, 1):
            kept = kept + over_head(sent[share_id - 1], share_id).astype(F32)
        return kept.astype(BF16)

    shares = [settle(0), settle(1)]
    low_keyval, low_gateq = project(gather(shares[0], "a"))
    low_other = over_ctx(low_keyval)
    high_keyval, high_gateq = project(gather(shares[1], "b"))
    high_other = over_ctx(high_keyval)
    low_first = near_part(0, [(0, 0)], [low_keyval], low_gateq)
    low_done = total(*attend(0, low_other, low_first, low_gateq, shares[0]))
    origins = [(0, 0), (0, 1), (1, 0)]
    high_first = near_part(1, origins, [low_keyval, low_other, high_keyval], high_gateq)
    high_done = total(*attend(1, high_other, high_first, high_gateq, shares[1]))
    both = jnp.stack([low_done, high_done]).reshape(2, 2, stripe, part)
    return jnp.where(own == 0, both, both[:, ::-1]).reshape(1, 2, rows, part)


def body(inputs, lengths, proj_in, proj_out):
    context_size = lax.axis_size("ctx")
    head_size = lax.axis_size("head")
    paired = context_size == 2 and inputs.shape[0] == 2 * context_size
    if paired and head_size == 4:
        return pair_body(inputs, lengths, proj_in, proj_out)
    return ring_body(inputs, lengths, proj_in, proj_out)


def solution(mesh):
    return jax.shard_map(
        body,
        mesh=mesh,
        in_specs=(P("dp", "ctx", "head"), P("dp"), P(None, None, "head"), P("head", None)),
        out_specs=P(("dp", "ctx"), None, None, "head"),
        check_vma=False,
    )
```

```python
import functools
import math

import jax
import jax.numpy as jnp
from jax import lax
from jax.experimental import pallas as pl
from jax.experimental.pallas import tpu as pltpu
from jax.sharding import PartitionSpec as P


HDIM = 128
GRANT = 8 << 20
GA, GB, RA, RB = ('spread', 'halving', 'halving', 'direct')
F32 = jnp.float32
BF16 = jnp.bfloat16


def layer_norm(values, epsilon):
    center = values - jnp.mean(values, axis=-1, keepdims=True)
    spread = jnp.mean(center * center, axis=-1, keepdims=True)
    return center * lax.rsqrt(spread + epsilon)


def silu_round(values):
    return jax.nn.silu(values).astype(jnp.bfloat16)


def ring_body(inputs, lengths, proj_in, proj_out):
    context_size = lax.axis_size("ctx")
    own_index = lax.axis_index("ctx")
    block_total, stripe, width_part = inputs.shape
    block_len = stripe * context_size
    row_count = 2 * block_len
    heads_dev = proj_in.shape[2] // HDIM
    reordered = jnp.stack([inputs[:context_size], inputs[context_size:][::-1]], axis=1)
    reordered = reordered.reshape(block_total, stripe, width_part)
    own_rows = lax.all_to_all(reordered, "ctx", split_axis=0, concat_axis=1, tiled=True)
    full_rows = lax.all_gather(own_rows, "head", axis=2, tiled=True)
    normed = layer_norm(full_rows.reshape(row_count, -1).astype(jnp.float32), 1e-06).astype(
        jnp.bfloat16
    )
    user_ends = jnp.cumsum(lengths)

    def segment(position):
        return jnp.sum((position[:, None] >= user_ends[None, :]).astype(jnp.int32), axis=1)

    offsets = jnp.arange(block_len, dtype=jnp.int32)
    own_blocks = jnp.stack([own_index, 2 * context_size - 1 - own_index])
    query_pos = (own_blocks[:, None] * block_len + offsets[None, :]).reshape(-1)
    query_seg = segment(query_pos)
    score_scale = 1.0 / math.sqrt(HDIM)
    projected = silu_round(
        jnp.einsum("rd,dgc->rgc", normed, proj_in, preferred_element_type=jnp.float32)
    )
    gating = projected[:, 0]
    queries = projected[:, 2]
    key_pair = (
        projected[:, 3].reshape(2, block_len, -1),
        projected[:, 1].reshape(2, block_len, -1),
    )

    def loader(shards, lead_row, tile_rows):
        key_rows = lax.dynamic_slice_in_dim(shards[0], lead_row, tile_rows, 0)
        value_rows = lax.dynamic_slice_in_dim(shards[1], lead_row, tile_rows, 0)
        return (
            key_rows.reshape(tile_rows * block_len, heads_dev, HDIM),
            value_rows.reshape(tile_rows * block_len, heads_dev, HDIM),
        )

    query_heads = queries.reshape(row_count, heads_dev, HDIM)
    zero_acc = jnp.zeros((row_count, heads_dev, HDIM), jnp.float32)
    shards = (
        lax.all_gather(key_pair[0], "ctx", axis=0, tiled=True),
        lax.all_gather(key_pair[1], "ctx", axis=0, tiled=True),
    )
    piece_rows = shards[0].shape[0]
    tile_rows = 4

    def one_tile(tile_index, partial_value):
        lead_row = tile_index * tile_rows
        listed = lead_row + jnp.arange(tile_rows, dtype=jnp.int32)
        holder = listed // 2
        block_ids = jnp.where(listed % 2 == 0, holder, 2 * context_size - 1 - holder)
        key_pos = (block_ids[:, None] * block_len + offsets[None, :]).reshape(-1)
        allowed = (query_seg[:, None] == segment(key_pos)[None, :]) & (
            key_pos[None, :] <= query_pos[:, None]
        )
        key_rows, value_rows = loader(shards, lead_row, tile_rows)
        scores = (
            jnp.einsum("qhd,khd->hqk", query_heads, key_rows, preferred_element_type=jnp.float32)
            * score_scale
        )
        weights = jnp.where(allowed[None], jax.nn.silu(scores), 0.0).astype(jnp.bfloat16)
        return partial_value + jnp.einsum(
            "hqk,khd->qhd", weights, value_rows, preferred_element_type=jnp.float32
        )

    attended = lax.fori_loop(0, piece_rows // tile_rows, one_tile, zero_acc)
    gate_prod = layer_norm(attended, 1e-05) * gating.reshape(row_count, heads_dev, HDIM).astype(
        jnp.float32
    )
    gate_prod = gate_prod.astype(jnp.bfloat16).reshape(row_count, -1)
    columns = lax.all_to_all(proj_out, "head", split_axis=1, concat_axis=0, tiled=True)
    summed = jnp.dot(
        lax.all_gather(gate_prod, "head", axis=1, tiled=True),
        columns,
        preferred_element_type=jnp.float32,
    )
    result = (own_rows.reshape(row_count, -1).astype(jnp.float32) + summed).astype(jnp.bfloat16)
    return result.reshape(1, 2, block_len, -1)


def half_silu(half):
    return half + half * jnp.tanh(half)


def project_kernel(ids, place, *refs):
    *shares, weight, keyval, gateq = refs
    pieces = [ref[k].astype(F32) for ref in shares for k in range(ref.shape[0])]
    if len(pieces) > len(ids):
        pieces[-2:] = [pieces[-2] + pieces[-1]]
    part = pieces[0].shape[1]
    width = part * len(pieces)
    mean = sum(jnp.sum(p, axis=1, keepdims=True) for p in pieces) / width
    pieces = [p - mean for p in pieces]
    spread = sum(jnp.sum(p * p, axis=1, keepdims=True) for p in pieces) / width
    rscale = lax.rsqrt(spread + 1e-06)
    acc = None
    for share_id, piece in zip(ids, pieces):
        lead = pl.multiple_of((place[1] ^ share_id) * part, part)
        term = jnp.dot(
            (piece * rscale).astype(BF16), weight[pl.ds(lead, part), :], preferred_element_type=F32
        )
        acc = term if acc is None else acc + term
    done = half_silu(acc * 0.5).astype(BF16)
    group = done.shape[1] // 4
    gateq[0] = done[:, :group]
    keyval[0] = done[:, group : 2 * group]
    gateq[1] = done[:, 2 * group : 3 * group]
    keyval[1] = done[:, 3 * group :]


def weighted_values(plan, place, lengths, gateq, keyvals, first=None):
    chunk, stripe, origins = plan
    rows, cols = gateq.shape[1:]

    def positions(shape, dim, which, side):
        offset = lax.broadcasted_iota(jnp.int32, shape, dim)
        if which == 0:
            return offset + side * stripe + jnp.where(offset < stripe, 0, stripe)
        inner = jnp.where(offset < stripe, offset + side * stripe, offset - side * stripe)
        return (3 - side) * rows + inner

    query_pos = positions((rows, 1), 0, chunk, place[0])
    start = jnp.zeros((rows, 1), jnp.int32)
    end = jnp.int32(0)
    for user in range(lengths.shape[0]):
        end = end + lengths[user]
        start = jnp.where(query_pos >= end, end, start)
    masks = []
    for which, side in origins:
        key_pos = positions((1, rows), 1, which, place[0] ^ side)
        masks.append((key_pos <= query_pos) & (key_pos >= start))
    scale = 0.5 / math.sqrt(HDIM)
    totals = []
    for head in range(cols // HDIM):
        lanes = slice(head * HDIM, (head + 1) * HDIM)
        query = gateq[1, :, lanes]
        total = None if first is None else first[:, lanes]
        for mask, ref in zip(masks, keyvals):
            scores = lax.dot_general(
                query, ref[1, :, lanes], (((1,), (1,)), ((), ())), preferred_element_type=F32
            )
            weights = jnp.where(mask, half_silu(scores * scale), 0.0).astype(BF16)
            term = jnp.dot(weights, ref[0, :, lanes], preferred_element_type=F32)
            total = term if total is None else total + term
        totals.append(total)
    return totals


def near_kernel(plan, place, lengths, *refs):
    *keyvals, gateq, partial = refs
    totals = weighted_values(plan, place, lengths, gateq, keyvals)
    for head, total in enumerate(totals):
        partial[:, head * HDIM : (head + 1) * HDIM] = total


def attend_kernel(plan, layout, place, lengths, keyval, partial, gateq, weight, share, *refs):
    *outputs, held = refs
    chunk, stripe, _ = plan
    part = share.shape[2]
    totals = weighted_values(plan, place, lengths, gateq, [keyval], partial)
    for head, total in enumerate(totals):
        lanes = slice(head * HDIM, (head + 1) * HDIM)
        total = total - jnp.mean(total, axis=1, keepdims=True)
        spread = jnp.mean(total * total, axis=1, keepdims=True)
        total = total * lax.rsqrt(spread + 1e-05)
        held[:, lanes] = (total * gateq[0, :, lanes].astype(F32)).astype(BF16)
    leads = [0, stripe]
    if chunk == 0:
        away = 1 - place[0]
        leads = [pl.multiple_of(away * stripe, stripe), pl.multiple_of((1 - away) * stripe, stripe)]
    gated = [held[pl.ds(lead, stripe), :] for lead in leads]
    shares = [share[0, pl.ds(lead, stripe), :] for lead in leads]
    if layout != "split":
        gated, shares = [jnp.concatenate(gated, axis=0)], [jnp.concatenate(shares, axis=0)]
    for index, (left, right) in enumerate(zip(gated, shares)):
        for share_id in (2, 3, 1, 0):
            lead = pl.multiple_of((place[1] ^ share_id) * part, part)
            product = jnp.dot(left, weight[:, pl.ds(lead, part)], preferred_element_type=F32)
            if share_id == 0:
                product = product + right.astype(F32)
            if layout == "direct":
                outputs[share_id][...] = product.astype(outputs[share_id].dtype)
            else:
                target = outputs[2 * index + 1 - (share_id & 1)]
                target[share_id >> 1] = product.astype(target.dtype)


def whole(memory_space=pltpu.VMEM):
    return pl.BlockSpec(memory_space=memory_space)


def pair_body(inputs, lengths, proj_in, proj_out):
    head_size = lax.axis_size("head")
    own = lax.axis_index("ctx")
    _, stripe, part = inputs.shape
    rows = 2 * stripe
    cols = proj_in.shape[2]
    place = jnp.stack([own, lax.axis_index("head")]).astype(jnp.int32)
    weight_in = proj_in.reshape(proj_in.shape[0], -1)

    def over_head(value, pairs):
        if isinstance(pairs, int):
            pairs = [(i, i ^ pairs) for i in range(head_size)]
        return lax.ppermute(value, "head", pairs)

    def over_ctx(value):
        return lax.ppermute(value, "ctx", [(0, 1), (1, 0)])

    def kernel_call(function, outs, args, scalars, cost, scratch=()):
        return pl.pallas_call(
            function,
            compiler_params=pltpu.CompilerParams(vmem_limit_bytes=GRANT),
            out_shape=tuple(jax.ShapeDtypeStruct(*out) for out in outs),
            in_specs=[whole(pltpu.SMEM)] * scalars + [whole()] * (len(args) - scalars),
            out_specs=tuple(whole() for _ in outs),
            scratch_shapes=scratch,
            cost_estimate=cost,
        )(*args)

    def cost(flops, transcendentals):
        return pl.CostEstimate(flops=flops, bytes_accessed=1 << 20, transcendentals=transcendentals)

    weights = []
    inner = [(1, 2), (2, 1)]
    outer = [(1, 0), (2, 3)]

    def gather(own_share, tag, way):
        far = over_head(own_share, 2)
        if tag == "a":
            after, weight = lax.optimization_barrier((far, weight_in))
            weights.append(weight)
        else:
            after = far
        if way == "halving":
            both = jnp.concatenate([own_share, after], axis=0)
            return (own_share, far, over_head(both, 1)), (0, 2, 1, 3)
        near = over_head(own_share, 1)
        mid = over_head(own_share, inner)
        relay = over_head(after, outer)
        return (own_share, near, far, mid, relay), (0, 1, 2, 3)

    def project(gathered):
        shares, ids = gathered
        size = ((2, rows, cols), BF16)
        return kernel_call(
            functools.partial(project_kernel, ids),
            (size, size),
            (place, *shares, weights[0]),
            1,
            cost(2 * rows * weight_in.size, rows * 4 * cols),
        )

    def near_part(chunk, origins, keyvals, gateq):
        count = len(keyvals)
        return kernel_call(
            functools.partial(near_kernel, (chunk, stripe, origins)),
            (((rows, cols), F32),),
            (place, lengths, *keyvals, gateq),
            2,
            cost(4 * rows * rows * cols * count, rows * rows * count * (cols // HDIM)),
        )[0]

    def attend(chunk, keyval, partial, gateq, share, layout):
        size = {"direct": (rows, part), "halving": (2, rows, part), "split": (2, stripe, part)}[layout]
        outs = ((size, BF16), (size, F32))
        outs = {
            "direct": (outs[1],) + outs[:1] * 3,
            "halving": outs,
            "split": outs * 2,
        }[layout]
        results = kernel_call(
            functools.partial(attend_kernel, (chunk, stripe, [(chunk, 1)]), layout),
            outs,
            (place, lengths, keyval, partial, gateq, proj_out, share),
            2,
            cost(4 * rows * rows * cols + 2 * rows * proj_out.size, rows * rows * (cols // HDIM)),
            [pltpu.VMEM((rows, cols), BF16)],
        )
        if layout == "direct":
            kept = results[0]
            for share_id in (2, 3, 1):
                come = over_head(results[share_id], share_id)
                kept = kept + come.astype(F32)
            return kept.astype(BF16)
        done = []
        for index in range(len(results) // 2):
            sent, kept = results[2 * index : 2 * index + 2]
            kept = kept + over_head(sent, 1).astype(F32)
            come = over_head(kept[1].astype(BF16), 2)
            done.append((kept[0] + come.astype(F32)).astype(BF16))
        return done[0] if len(done) == 1 else jnp.concatenate(done, axis=0)

    low = inputs[:2].reshape(1, rows, part)
    home = lax.dynamic_index_in_dim(inputs[2:], 1 - own, 0, keepdims=True)
    away = lax.dynamic_index_in_dim(inputs[2:], own, 0, keepdims=True)
    high = jnp.concatenate([home, over_ctx(away)], axis=1)
    low_keyval, low_gateq = project(gather(low, "a", GA))
    low_other = over_ctx(low_keyval)
    high_keyval, high_gateq = project(gather(high, "b", GB))
    high_other = over_ctx(high_keyval)
    low_first = near_part(0, [(0, 0)], [low_keyval], low_gateq)
    low_done = attend(0, low_other, low_first, low_gateq, low, RA)
    origins = [(0, 0), (0, 1), (1, 0)]
    high_first = near_part(1, origins, [low_keyval, low_other, high_keyval], high_gateq)
    high_done = attend(1, high_other, high_first, high_gateq, high, RB)
    come = over_ctx(low_done[:stripe])
    both = jnp.concatenate([low_done[stripe:], come, high_done], axis=0).reshape(2, 2, stripe, part)
    return jnp.where(own == 0, both, both[:, ::-1]).reshape(1, 2, rows, part)


def body(inputs, lengths, proj_in, proj_out):
    context_size = lax.axis_size("ctx")
    head_size = lax.axis_size("head")
    paired = context_size == 2 and inputs.shape[0] == 2 * context_size
    if paired and head_size == 4:
        return pair_body(inputs, lengths, proj_in, proj_out)
    return ring_body(inputs, lengths, proj_in, proj_out)


def solution(mesh):
    return jax.shard_map(
        body,
        mesh=mesh,
        in_specs=(P("dp", "ctx", "head"), P("dp"), P(None, None, "head"), P("head", None)),
        out_specs=P(("dp", "ctx"), None, None, "head"),
        check_vma=False,
    )
```

```python
import functools
import math

import jax
import jax.numpy as jnp
from jax import lax
from jax.experimental import pallas as pl
from jax.experimental.pallas import tpu as pltpu
from jax.sharding import PartitionSpec as P


HDIM = 128
GRANT = 8 << 20
F32 = jnp.float32
BF16 = jnp.bfloat16


def layer_norm(values, epsilon):
    center = values - jnp.mean(values, axis=-1, keepdims=True)
    spread = jnp.mean(center * center, axis=-1, keepdims=True)
    return center * lax.rsqrt(spread + epsilon)


def silu_round(values):
    return jax.nn.silu(values).astype(jnp.bfloat16)


def ring_body(inputs, lengths, proj_in, proj_out):
    context_size = lax.axis_size("ctx")
    own_index = lax.axis_index("ctx")
    block_total, stripe, width_part = inputs.shape
    block_len = stripe * context_size
    row_count = 2 * block_len
    heads_dev = proj_in.shape[2] // HDIM
    reordered = jnp.stack([inputs[:context_size], inputs[context_size:][::-1]], axis=1)
    reordered = reordered.reshape(block_total, stripe, width_part)
    own_rows = lax.all_to_all(reordered, "ctx", split_axis=0, concat_axis=1, tiled=True)
    full_rows = lax.all_gather(own_rows, "head", axis=2, tiled=True)
    normed = layer_norm(full_rows.reshape(row_count, -1).astype(jnp.float32), 1e-06).astype(
        jnp.bfloat16
    )
    user_ends = jnp.cumsum(lengths)

    def segment(position):
        return jnp.sum((position[:, None] >= user_ends[None, :]).astype(jnp.int32), axis=1)

    offsets = jnp.arange(block_len, dtype=jnp.int32)
    own_blocks = jnp.stack([own_index, 2 * context_size - 1 - own_index])
    query_pos = (own_blocks[:, None] * block_len + offsets[None, :]).reshape(-1)
    query_seg = segment(query_pos)
    score_scale = 1.0 / math.sqrt(HDIM)
    projected = silu_round(
        jnp.einsum("rd,dgc->rgc", normed, proj_in, preferred_element_type=jnp.float32)
    )
    gating = projected[:, 0]
    queries = projected[:, 2]
    key_pair = (
        projected[:, 3].reshape(2, block_len, -1),
        projected[:, 1].reshape(2, block_len, -1),
    )

    def loader(shards, lead_row, tile_rows):
        key_rows = lax.dynamic_slice_in_dim(shards[0], lead_row, tile_rows, 0)
        value_rows = lax.dynamic_slice_in_dim(shards[1], lead_row, tile_rows, 0)
        return (
            key_rows.reshape(tile_rows * block_len, heads_dev, HDIM),
            value_rows.reshape(tile_rows * block_len, heads_dev, HDIM),
        )

    query_heads = queries.reshape(row_count, heads_dev, HDIM)
    zero_acc = jnp.zeros((row_count, heads_dev, HDIM), jnp.float32)
    shards = (
        lax.all_gather(key_pair[0], "ctx", axis=0, tiled=True),
        lax.all_gather(key_pair[1], "ctx", axis=0, tiled=True),
    )
    piece_rows = shards[0].shape[0]
    tile_rows = 4

    def one_tile(tile_index, partial_value):
        lead_row = tile_index * tile_rows
        listed = lead_row + jnp.arange(tile_rows, dtype=jnp.int32)
        holder = listed // 2
        block_ids = jnp.where(listed % 2 == 0, holder, 2 * context_size - 1 - holder)
        key_pos = (block_ids[:, None] * block_len + offsets[None, :]).reshape(-1)
        allowed = (query_seg[:, None] == segment(key_pos)[None, :]) & (
            key_pos[None, :] <= query_pos[:, None]
        )
        key_rows, value_rows = loader(shards, lead_row, tile_rows)
        scores = (
            jnp.einsum("qhd,khd->hqk", query_heads, key_rows, preferred_element_type=jnp.float32)
            * score_scale
        )
        weights = jnp.where(allowed[None], jax.nn.silu(scores), 0.0).astype(jnp.bfloat16)
        return partial_value + jnp.einsum(
            "hqk,khd->qhd", weights, value_rows, preferred_element_type=jnp.float32
        )

    attended = lax.fori_loop(0, piece_rows // tile_rows, one_tile, zero_acc)
    gate_prod = layer_norm(attended, 1e-05) * gating.reshape(row_count, heads_dev, HDIM).astype(
        jnp.float32
    )
    gate_prod = gate_prod.astype(jnp.bfloat16).reshape(row_count, -1)
    columns = lax.all_to_all(proj_out, "head", split_axis=1, concat_axis=0, tiled=True)
    summed = jnp.dot(
        lax.all_gather(gate_prod, "head", axis=1, tiled=True),
        columns,
        preferred_element_type=jnp.float32,
    )
    result = (own_rows.reshape(row_count, -1).astype(jnp.float32) + summed).astype(jnp.bfloat16)
    return result.reshape(1, 2, block_len, -1)


def half_silu(half):
    return half + half * jnp.tanh(half)


def project_kernel(ids, groups, *refs):
    *shares, weight, target = refs
    pieces = [ref[k].astype(F32) for ref in shares for k in range(ref.shape[0])]
    if len(pieces) > len(ids):
        pieces[-2:] = [pieces[-2] + pieces[-1]]
    part, size = pieces[0].shape[1], target.shape[2]
    width = part * len(pieces)
    mean = sum(jnp.sum(p, axis=1, keepdims=True) for p in pieces) / width
    pieces = [p - mean for p in pieces]
    spread = sum(jnp.sum(p * p, axis=1, keepdims=True) for p in pieces) / width
    rscale = lax.rsqrt(spread + 1e-06)
    pieces = [(p * rscale).astype(BF16) for p in pieces]
    head = lax.axis_index("head")
    for slot, group in enumerate(groups):
        lanes = slice(group * size, (group + 1) * size)
        acc = None
        for share_id, piece in zip(ids, pieces):
            lead = pl.multiple_of((head ^ share_id) * part, part)
            term = jnp.dot(piece, weight[pl.ds(lead, part), lanes], preferred_element_type=F32)
            acc = term if acc is None else acc + term
        target[slot] = half_silu(acc * 0.5).astype(BF16)


def positions(offset, which, side, stripe):
    if which == 0:
        return offset + side * stripe + jnp.where(offset < stripe, 0, stripe)
    inner = jnp.where(offset < stripe, offset + side * stripe, offset - side * stripe)
    return (3 - side) * 2 * stripe + inner


def weighted_values(plan, lengths, gateq, keyvals, first=None):
    chunk, stripe, origins = plan
    rows, cols = gateq.shape[1:]
    own = lax.axis_index("ctx")
    query_pos = positions(lax.broadcasted_iota(jnp.int32, (rows, HDIM), 0), chunk, own, stripe)
    start = jnp.zeros((rows, HDIM), jnp.int32)
    end = jnp.zeros((1, HDIM), jnp.int32)
    for user in range(lengths.shape[0]):
        end = end + lengths[user : user + 1, :]
        start = jnp.where(query_pos >= end, end, start)
    query_pos = jnp.concatenate([query_pos] * (rows // HDIM), axis=1)
    lowest = jnp.concatenate([start] * (rows // HDIM), axis=1)
    masks = []
    for which, side in origins:
        offset = lax.broadcasted_iota(jnp.int32, (1, rows), 1)
        key_pos = positions(offset, which, own ^ side, stripe)
        masks.append((key_pos <= query_pos) & (key_pos >= lowest))
    scale = 0.5 / math.sqrt(HDIM)
    totals = []
    for head in range(cols // HDIM):
        lanes = slice(head * HDIM, (head + 1) * HDIM)
        query = gateq[1, :, lanes]
        total = None if first is None else first[:, lanes]
        for mask, ref in zip(masks, keyvals):
            scores = lax.dot_general(
                query, ref[1, :, lanes], (((1,), (1,)), ((), ())), preferred_element_type=F32
            )
            weights = jnp.where(mask, half_silu(scores * scale), 0.0).astype(BF16)
            term = jnp.dot(weights, ref[0, :, lanes], preferred_element_type=F32)
            total = term if total is None else total + term
        totals.append(total)
    return totals


def near_kernel(plan, lengths, *refs):
    *keyvals, gateq, partial = refs
    totals = weighted_values(plan, lengths, gateq, keyvals)
    for head, total in enumerate(totals):
        partial[:, head * HDIM : (head + 1) * HDIM] = total


def attend_kernel(plan, lengths, keyval, partial, gateq, weight, share, *refs):
    *outputs, held = refs
    chunk, stripe, _ = plan
    part = share.shape[2]
    totals = weighted_values(plan, lengths, gateq, [keyval], partial)
    for head, total in enumerate(totals):
        lanes = slice(head * HDIM, (head + 1) * HDIM)
        total = total - jnp.mean(total, axis=1, keepdims=True)
        spread = jnp.mean(total * total, axis=1, keepdims=True)
        total = total * lax.rsqrt(spread + 1e-05)
        held[:, lanes] = (total * gateq[0, :, lanes].astype(F32)).astype(BF16)
    leads = [0, stripe]
    if chunk == 0:
        away = 1 - lax.axis_index("ctx")
        leads = [pl.multiple_of(away * stripe, stripe), pl.multiple_of((1 - away) * stripe, stripe)]
    gated = jnp.concatenate([held[pl.ds(lead, stripe), :] for lead in leads], axis=0)
    share = jnp.concatenate([share[0, pl.ds(lead, stripe), :] for lead in leads], axis=0)
    for share_id in (2, 3, 1, 0):
        lead = pl.multiple_of((lax.axis_index("head") ^ share_id) * part, part)
        product = jnp.dot(gated, weight[:, pl.ds(lead, part)], preferred_element_type=F32)
        if share_id == 0:
            product = product + share.astype(F32)
        outputs[share_id][...] = product.astype(outputs[share_id].dtype)


def whole():
    return pl.BlockSpec(memory_space=pltpu.VMEM)


def pair_body(inputs, lengths, proj_in, proj_out):
    head_size = lax.axis_size("head")
    own = lax.axis_index("ctx")
    _, stripe, part = inputs.shape
    rows = 2 * stripe
    cols = proj_in.shape[2]
    lengths = jnp.broadcast_to(lengths[:, None], (lengths.shape[0], HDIM))
    weight_in = proj_in.reshape(proj_in.shape[0], -1)

    def over_head(value, pairs):
        if isinstance(pairs, int):
            pairs = [(i, i ^ pairs) for i in range(head_size)]
        return lax.ppermute(value, "head", pairs)

    def over_ctx(value):
        return lax.ppermute(value, "ctx", [(0, 1), (1, 0)])

    def kernel_call(function, outs, args, cost, scratch=()):
        return pl.pallas_call(
            function,
            compiler_params=pltpu.CompilerParams(vmem_limit_bytes=GRANT),
            out_shape=tuple(jax.ShapeDtypeStruct(*out) for out in outs),
            in_specs=[whole() for _ in args],
            out_specs=tuple(whole() for _ in outs),
            scratch_shapes=scratch,
            cost_estimate=cost,
        )(*args)

    def cost(flops, transcendentals):
        return pl.CostEstimate(flops=flops, bytes_accessed=1 << 20, transcendentals=transcendentals)

    weights = []
    inner = [(1, 2), (2, 1)]
    outer = [(1, 0), (2, 3)]

    def gather(own_share, tag):
        far = over_head(own_share, 2)
        after = far
        if tag == "a":
            after, weight = lax.optimization_barrier((far, weight_in))
            weights.append(weight)
        near = over_head(own_share, 1)
        mid = over_head(own_share, inner)
        relay = over_head(after, outer)
        return own_share, near, far, mid, relay

    def project(shares, groups):
        return kernel_call(
            functools.partial(project_kernel, range(head_size), groups),
            (((2, rows, cols), BF16),),
            (*shares, weights[0]),
            cost(rows * weight_in.size, rows * 2 * cols),
        )[0]

    def near_part(chunk, origins, keyvals, gateq):
        count = len(keyvals)
        return kernel_call(
            functools.partial(near_kernel, (chunk, stripe, origins)),
            (((rows, cols), F32),),
            (lengths, *keyvals, gateq),
            cost(4 * rows * rows * cols * count, rows * rows * count * (cols // HDIM)),
        )[0]

    def attend(chunk, keyval, partial, gateq, share):
        return kernel_call(
            functools.partial(attend_kernel, (chunk, stripe, [(chunk, 1)])),
            (((rows, part), F32),) + (((rows, part), BF16),) * 3,
            (lengths, keyval, partial, gateq, proj_out, share),
            cost(4 * rows * rows * cols + 2 * rows * proj_out.size, rows * rows * (cols // HDIM)),
            [pltpu.VMEM((rows, cols), BF16)],
        )

    def total_relayed(kept, near, far, last):
        given = over_head(last, [(0, 1), (3, 2)])
        for come in (over_head(last, inner), over_head(near, 1), over_head(far + given, 2)):
            kept = kept + come.astype(F32)
        return kept.astype(BF16)

    def total_direct(kept, *sent):
        for share_id in (2, 3, 1):
            come = over_head(sent[share_id - 1], share_id)
            kept = kept + come.astype(F32)
        return kept.astype(BF16)

    flag = lax.optimization_barrier(jnp.full((1, part), own, jnp.int32))
    low = inputs[:2].reshape(1, rows, part)
    home = lax.dynamic_index_in_dim(inputs[2:], 1 - own, 0, keepdims=True)
    away = lax.dynamic_index_in_dim(inputs[2:], own, 0, keepdims=True)
    high = jnp.concatenate([home, over_ctx(away)], axis=1)
    low_shares = gather(low, "a")
    low_keyval = project(low_shares, (1, 3))
    low_other = over_ctx(low_keyval)
    low_gateq = project(low_shares, (0, 2))
    high_shares = gather(high, "b")
    high_keyval = project(high_shares, (1, 3))
    high_other = over_ctx(high_keyval)
    high_gateq = project(high_shares, (0, 2))
    low_first = near_part(0, [(0, 0)], [low_keyval], low_gateq)
    low_done = total_relayed(*attend(0, low_other, low_first, low_gateq, low))
    origins = [(0, 0), (0, 1), (1, 0)]
    high_first = near_part(1, origins, [low_keyval, low_other, high_keyval], high_gateq)
    high_done = total_direct(*attend(1, high_other, high_first, high_gateq, high))
    come = over_ctx(low_done[:stripe])
    both = jnp.concatenate([low_done[stripe:], come, high_done], axis=0).reshape(2, 2, stripe, part)
    return jnp.where(flag == 0, both, both[:, ::-1]).reshape(1, 2, rows, part)


def body(inputs, lengths, proj_in, proj_out):
    context_size = lax.axis_size("ctx")
    head_size = lax.axis_size("head")
    paired = context_size == 2 and inputs.shape[0] == 2 * context_size
    if paired and head_size == 4:
        return pair_body(inputs, lengths, proj_in, proj_out)
    return ring_body(inputs, lengths, proj_in, proj_out)


def solution(mesh):
    return jax.shard_map(
        body,
        mesh=mesh,
        in_specs=(P("dp", "ctx", "head"), P("dp"), P(None, None, "head"), P("head", None)),
        out_specs=P(("dp", "ctx"), None, None, "head"),
        check_vma=False,
    )
```

```python
import functools
import math

import jax
import jax.numpy as jnp
from jax import lax
from jax.experimental import pallas as pl
from jax.experimental.pallas import tpu as pltpu
from jax.sharding import PartitionSpec as P


HDIM = 128
GRANT = 8 << 20
F32 = jnp.float32
BF16 = jnp.bfloat16


def layer_norm(values, epsilon):
    center = values - jnp.mean(values, axis=-1, keepdims=True)
    spread = jnp.mean(center * center, axis=-1, keepdims=True)
    return center * lax.rsqrt(spread + epsilon)


def silu_round(values):
    return jax.nn.silu(values).astype(jnp.bfloat16)


def ring_body(inputs, lengths, proj_in, proj_out):
    context_size = lax.axis_size("ctx")
    own_index = lax.axis_index("ctx")
    block_total, stripe, width_part = inputs.shape
    block_len = stripe * context_size
    row_count = 2 * block_len
    heads_dev = proj_in.shape[2] // HDIM
    reordered = jnp.stack([inputs[:context_size], inputs[context_size:][::-1]], axis=1)
    reordered = reordered.reshape(block_total, stripe, width_part)
    own_rows = lax.all_to_all(reordered, "ctx", split_axis=0, concat_axis=1, tiled=True)
    full_rows = lax.all_gather(own_rows, "head", axis=2, tiled=True)
    normed = layer_norm(full_rows.reshape(row_count, -1).astype(jnp.float32), 1e-06).astype(
        jnp.bfloat16
    )
    user_ends = jnp.cumsum(lengths)

    def segment(position):
        return jnp.sum((position[:, None] >= user_ends[None, :]).astype(jnp.int32), axis=1)

    offsets = jnp.arange(block_len, dtype=jnp.int32)
    own_blocks = jnp.stack([own_index, 2 * context_size - 1 - own_index])
    query_pos = (own_blocks[:, None] * block_len + offsets[None, :]).reshape(-1)
    query_seg = segment(query_pos)
    score_scale = 1.0 / math.sqrt(HDIM)
    projected = silu_round(
        jnp.einsum("rd,dgc->rgc", normed, proj_in, preferred_element_type=jnp.float32)
    )
    gating = projected[:, 0]
    queries = projected[:, 2]
    key_pair = (
        projected[:, 3].reshape(2, block_len, -1),
        projected[:, 1].reshape(2, block_len, -1),
    )

    def loader(shards, lead_row, tile_rows):
        key_rows = lax.dynamic_slice_in_dim(shards[0], lead_row, tile_rows, 0)
        value_rows = lax.dynamic_slice_in_dim(shards[1], lead_row, tile_rows, 0)
        return (
            key_rows.reshape(tile_rows * block_len, heads_dev, HDIM),
            value_rows.reshape(tile_rows * block_len, heads_dev, HDIM),
        )

    query_heads = queries.reshape(row_count, heads_dev, HDIM)
    zero_acc = jnp.zeros((row_count, heads_dev, HDIM), jnp.float32)
    shards = (
        lax.all_gather(key_pair[0], "ctx", axis=0, tiled=True),
        lax.all_gather(key_pair[1], "ctx", axis=0, tiled=True),
    )
    piece_rows = shards[0].shape[0]
    tile_rows = 4

    def one_tile(tile_index, partial_value):
        lead_row = tile_index * tile_rows
        listed = lead_row + jnp.arange(tile_rows, dtype=jnp.int32)
        holder = listed // 2
        block_ids = jnp.where(listed % 2 == 0, holder, 2 * context_size - 1 - holder)
        key_pos = (block_ids[:, None] * block_len + offsets[None, :]).reshape(-1)
        allowed = (query_seg[:, None] == segment(key_pos)[None, :]) & (
            key_pos[None, :] <= query_pos[:, None]
        )
        key_rows, value_rows = loader(shards, lead_row, tile_rows)
        scores = (
            jnp.einsum("qhd,khd->hqk", query_heads, key_rows, preferred_element_type=jnp.float32)
            * score_scale
        )
        weights = jnp.where(allowed[None], jax.nn.silu(scores), 0.0).astype(jnp.bfloat16)
        return partial_value + jnp.einsum(
            "hqk,khd->qhd", weights, value_rows, preferred_element_type=jnp.float32
        )

    attended = lax.fori_loop(0, piece_rows // tile_rows, one_tile, zero_acc)
    gate_prod = layer_norm(attended, 1e-05) * gating.reshape(row_count, heads_dev, HDIM).astype(
        jnp.float32
    )
    gate_prod = gate_prod.astype(jnp.bfloat16).reshape(row_count, -1)
    columns = lax.all_to_all(proj_out, "head", split_axis=1, concat_axis=0, tiled=True)
    summed = jnp.dot(
        lax.all_gather(gate_prod, "head", axis=1, tiled=True),
        columns,
        preferred_element_type=jnp.float32,
    )
    result = (own_rows.reshape(row_count, -1).astype(jnp.float32) + summed).astype(jnp.bfloat16)
    return result.reshape(1, 2, block_len, -1)


def half_silu(half):
    return half + half * jnp.tanh(half)


def project_kernel(ids, groups, *refs):
    *shares, weight, target = refs
    pieces = [ref[k].astype(F32) for ref in shares for k in range(ref.shape[0])]
    part, size = pieces[0].shape[1], target.shape[2]
    width = part * len(pieces)
    mean = sum(jnp.sum(p, axis=1, keepdims=True) for p in pieces) / width
    pieces = [p - mean for p in pieces]
    spread = sum(jnp.sum(p * p, axis=1, keepdims=True) for p in pieces) / width
    rscale = lax.rsqrt(spread + 1e-06)
    pieces = [(p * rscale).astype(BF16) for p in pieces]
    head = lax.axis_index("head")
    for slot, group in enumerate(groups):
        lanes = slice(group * size, (group + 1) * size)
        acc = None
        for share_id, piece in zip(ids, pieces):
            lead = pl.multiple_of((head ^ share_id) * part, part)
            term = jnp.dot(piece, weight[pl.ds(lead, part), lanes], preferred_element_type=F32)
            acc = term if acc is None else acc + term
        target[slot] = half_silu(acc * 0.5).astype(BF16)


def positions(offset, which, side, stripe):
    if which == 0:
        return offset + side * stripe + jnp.where(offset < stripe, 0, stripe)
    inner = jnp.where(offset < stripe, offset + side * stripe, offset - side * stripe)
    return (3 - side) * 2 * stripe + inner


def weighted_values(plan, lengths, gateq, keyvals, first=None):
    chunk, stripe, origins = plan
    rows, cols = gateq.shape[1:]
    own = lax.axis_index("ctx")
    query_pos = positions(lax.broadcasted_iota(jnp.int32, (rows, HDIM), 0), chunk, own, stripe)
    start = jnp.zeros((rows, HDIM), jnp.int32)
    end = jnp.zeros((1, HDIM), jnp.int32)
    for user in range(lengths.shape[0]):
        end = end + lengths[user : user + 1, :]
        start = jnp.where(query_pos >= end, end, start)
    query_pos = jnp.concatenate([query_pos] * (rows // HDIM), axis=1)
    lowest = jnp.concatenate([start] * (rows // HDIM), axis=1)
    masks = []
    for which, side in origins:
        offset = lax.broadcasted_iota(jnp.int32, (1, rows), 1)
        key_pos = positions(offset, which, own ^ side, stripe)
        masks.append((key_pos <= query_pos) & (key_pos >= lowest))
    scale = 0.5 / math.sqrt(HDIM)
    totals = []
    for head in range(cols // HDIM):
        lanes = slice(head * HDIM, (head + 1) * HDIM)
        query = gateq[1, :, lanes]
        total = None if first is None else first[:, lanes]
        for mask, ref in zip(masks, keyvals):
            scores = lax.dot_general(
                query, ref[1, :, lanes], (((1,), (1,)), ((), ())), preferred_element_type=F32
            )
            weights = jnp.where(mask, half_silu(scores * scale), 0.0).astype(BF16)
            term = jnp.dot(weights, ref[0, :, lanes], preferred_element_type=F32)
            total = term if total is None else total + term
        totals.append(total)
    return totals


def near_kernel(plan, lengths, *refs):
    *keyvals, gateq, partial = refs
    totals = weighted_values(plan, lengths, gateq, keyvals)
    for head, total in enumerate(totals):
        partial[:, head * HDIM : (head + 1) * HDIM] = total


def attend_kernel(plan, lengths, keyval, partial, gateq, weight, share, *refs):
    *outputs, held = refs
    chunk, stripe, _ = plan
    part = share.shape[2]
    totals = weighted_values(plan, lengths, gateq, [keyval], partial)
    for head, total in enumerate(totals):
        lanes = slice(head * HDIM, (head + 1) * HDIM)
        total = total - jnp.mean(total, axis=1, keepdims=True)
        spread = jnp.mean(total * total, axis=1, keepdims=True)
        total = total * lax.rsqrt(spread + 1e-05)
        held[:, lanes] = (total * gateq[0, :, lanes].astype(F32)).astype(BF16)
    leads = [0, stripe]
    if chunk == 0:
        away = 1 - lax.axis_index("ctx")
        leads = [pl.multiple_of(away * stripe, stripe), pl.multiple_of((1 - away) * stripe, stripe)]
    gated = jnp.concatenate([held[pl.ds(lead, stripe), :] for lead in leads], axis=0)
    share = jnp.concatenate([share[0, pl.ds(lead, stripe), :] for lead in leads], axis=0)
    for share_id in (2, 3, 1, 0):
        lead = pl.multiple_of((lax.axis_index("head") ^ share_id) * part, part)
        product = jnp.dot(gated, weight[:, pl.ds(lead, part)], preferred_element_type=F32)
        if share_id == 0:
            product = product + share.astype(F32)
        outputs[share_id][...] = product.astype(outputs[share_id].dtype)


def whole():
    return pl.BlockSpec(memory_space=pltpu.VMEM)


def pair_body(inputs, lengths, proj_in, proj_out):
    head_size = lax.axis_size("head")
    own = lax.axis_index("ctx")
    _, stripe, part = inputs.shape
    rows = 2 * stripe
    cols = proj_in.shape[2]
    lengths = jnp.broadcast_to(lengths[:, None], (lengths.shape[0], HDIM))
    weight_in = proj_in.reshape(proj_in.shape[0], -1)

    def over_head(value, pairs):
        if isinstance(pairs, int):
            pairs = [(i, i ^ pairs) for i in range(head_size)]
        return lax.ppermute(value, "head", pairs)

    def over_ctx(value):
        return lax.ppermute(value, "ctx", [(0, 1), (1, 0)])

    def kernel_call(function, outs, args, cost, scratch=()):
        return pl.pallas_call(
            function,
            compiler_params=pltpu.CompilerParams(vmem_limit_bytes=GRANT),
            out_shape=tuple(jax.ShapeDtypeStruct(*out) for out in outs),
            in_specs=[whole() for _ in args],
            out_specs=tuple(whole() for _ in outs),
            scratch_shapes=scratch,
            cost_estimate=cost,
        )(*args)

    def cost(flops, transcendentals):
        return pl.CostEstimate(flops=flops, bytes_accessed=1 << 20, transcendentals=transcendentals)

    inner = [(1, 2), (2, 1)]

    def gather(own_share):
        return (own_share,) + tuple(over_head(own_share, share_id) for share_id in (1, 2, 3))

    def project(shares, groups):
        return kernel_call(
            functools.partial(project_kernel, range(head_size), groups),
            (((2, rows, cols), BF16),),
            (*shares, weight_in),
            cost(rows * weight_in.size, rows * 2 * cols),
        )[0]

    def near_part(chunk, origins, keyvals, gateq):
        count = len(keyvals)
        return kernel_call(
            functools.partial(near_kernel, (chunk, stripe, origins)),
            (((rows, cols), F32),),
            (lengths, *keyvals, gateq),
            cost(4 * rows * rows * cols * count, rows * rows * count * (cols // HDIM)),
        )[0]

    def attend(chunk, keyval, partial, gateq, share):
        return kernel_call(
            functools.partial(attend_kernel, (chunk, stripe, [(chunk, 1)])),
            (((rows, part), F32),) + (((rows, part), BF16),) * 3,
            (lengths, keyval, partial, gateq, proj_out, share),
            cost(4 * rows * rows * cols + 2 * rows * proj_out.size, rows * rows * (cols // HDIM)),
            [pltpu.VMEM((rows, cols), BF16)],
        )

    def total_relayed(kept, near, far, last):
        given = over_head(last, [(0, 1), (3, 2)])
        for come in (over_head(last, inner), over_head(near, 1), over_head(far + given, 2)):
            kept = kept + come.astype(F32)
        return kept.astype(BF16)

    def total_direct(kept, *sent):
        for share_id in (2, 3, 1):
            come = over_head(sent[share_id - 1], share_id)
            kept = kept + come.astype(F32)
        return kept.astype(BF16)

    flag = lax.optimization_barrier(jnp.full((1, part), own, jnp.int32))
    low = inputs[:2].reshape(1, rows, part)
    home = lax.dynamic_index_in_dim(inputs[2:], 1 - own, 0, keepdims=True)
    away = lax.dynamic_index_in_dim(inputs[2:], own, 0, keepdims=True)
    high = jnp.concatenate([home, over_ctx(away)], axis=1)
    low_shares = gather(low)
    low_keyval = project(low_shares, (1, 3))
    low_other = over_ctx(low_keyval)
    low_gateq = project(low_shares, (0, 2))
    high_shares = gather(high)
    high_keyval = project(high_shares, (1, 3))
    high_other = over_ctx(high_keyval)
    high_gateq = project(high_shares, (0, 2))
    low_first = near_part(0, [(0, 0)], [low_keyval], low_gateq)
    low_done = total_relayed(*attend(0, low_other, low_first, low_gateq, low))
    origins = [(0, 0), (0, 1), (1, 0)]
    high_first = near_part(1, origins, [low_keyval, low_other, high_keyval], high_gateq)
    high_done = total_direct(*attend(1, high_other, high_first, high_gateq, high))
    come = over_ctx(low_done[:stripe])
    both = jnp.concatenate([low_done[stripe:], come, high_done], axis=0).reshape(2, 2, stripe, part)
    return jnp.where(flag == 0, both, both[:, ::-1]).reshape(1, 2, rows, part)


def body(inputs, lengths, proj_in, proj_out):
    context_size = lax.axis_size("ctx")
    head_size = lax.axis_size("head")
    paired = context_size == 2 and inputs.shape[0] == 2 * context_size
    if paired and head_size == 4:
        return pair_body(inputs, lengths, proj_in, proj_out)
    return ring_body(inputs, lengths, proj_in, proj_out)


def solution(mesh):
    return jax.shard_map(
        body,
        mesh=mesh,
        in_specs=(P("dp", "ctx", "head"), P("dp"), P(None, None, "head"), P("head", None)),
        out_specs=P(("dp", "ctx"), None, None, "head"),
        check_vma=False,
    )
```
